256 devices in a mesh: section: 4 (over x), tm: 64 (over y, z, core).
Axes of the slice: x: 4, y: 4, z: 8, core: 2. Of those that a mesh axis runs over, the one named last changes fastest.
Arguments:
- signal: bfloat16 [4, 32768, 256], P(None, 'tm'), may hold values from -6 to 6
- skip_cot: bfloat16 [4, 32768, 256], P(None, 'tm'), may hold values from -6 to 6
- res_cot: bfloat16 [4, 32768, 256], P(None, 'tm'), may hold values from -6 to 6
- w_tap: bfloat16 [4, 256, 512], P('section'), may hold values from -0.25 to 0.25
- w_now: bfloat16 [4, 256, 512], P('section'), may hold values from -0.25 to 0.25
- w_res: bfloat16 [4, 256, 256], P('section'), may hold values from -0.375 to 0.375
- w_skip: bfloat16 [4, 256, 256], P('section'), may hold values from -0.375 to 0.375
Outputs:
- skip_total: bfloat16 [4, 32768, 256], P(None, 'tm')
- input_grads: bfloat16 [4, 4, 32768, 256], P('section', None, 'tm')
- grad_tap: float32 [4, 256, 512], P('section')
- grad_now: float32 [4, 256, 512], P('section')
- grad_res: float32 [4, 256, 256], P('section')
- grad_skip: float32 [4, 256, 256], P('section')
The draws below stay inside these ranges and needn't reach their ends.
All inputs are finite; a program needn't handle non-finite values.
Results may differ from the reference program's by a relative error of at most 0.01.
Values may be sent and summed in bfloat16 or wider, within the bound.
A program may use at most 64 MiB of HBM per device.

```python
import math
import jax
import jax.numpy as jnp

C = 256
GATE = 512
SKIP = 256
B = 4
HALF = 256
LAYERS = 4
L = 32768
FIRST_DILATION = 2048


def levels(rng, extent, split, low, largest):
    gain, own = 1.0, jax.random.fold_in(rng, 6)
    for dim, shards_of in split:
        heights = jnp.exp(jax.random.uniform(jax.random.fold_in(own, dim), (shards_of,), jnp.float32, low / len(split), largest / len(split)))
        gain = gain * jnp.repeat(heights, extent[dim] // shards_of).reshape([-1 if axis == dim else 1 for axis in range(len(extent))])
    return gain


def gaussian(key, dims, spread, limit, shards=(), held_as=jnp.bfloat16):
    gain = levels(key, dims, shards, -0.22, 0.18) if shards else 1.0
    entries = jax.random.normal(key, dims, jnp.float32) * spread * gain
    return jnp.minimum(jnp.maximum(entries, -limit), limit).astype(held_as)


def setup_inputs(seed: int = 0) -> dict:
    key_of = jax.random.split(jax.random.key(seed), 8)
    signal = gaussian(key_of[0], (B, L, C), 1.0, 6.0, ((1, 64),))
    skip_cot = gaussian(key_of[1], (B, L, SKIP), 1.0, 6.0, ((1, 64),))
    res_cot = gaussian(key_of[2], (B, L, C), 1.0, 6.0, ((1, 64),))
    w_tap = gaussian(key_of[3], (LAYERS, C, GATE), (2 * C) ** -0.5, 0.25, ((0, 4),))
    w_now = gaussian(key_of[4], (LAYERS, C, GATE), (2 * C) ** -0.5, 0.25, ((0, 4),))
    w_res = gaussian(key_of[5], (LAYERS, HALF, C), HALF ** -0.5, 0.375, ((0, 4),))
    w_skip = gaussian(key_of[6], (LAYERS, HALF, SKIP), HALF ** -0.5, 0.375, ((0, 4),))
    return {"signal": signal, "skip_cot": skip_cot, "res_cot": res_cot, "w_tap": w_tap, "w_now": w_now, "w_res": w_res, "w_skip": w_skip}


def delayed_rows(values, dilation_offset):
    padded = jnp.pad(values, ((dilation_offset, 0), (0, 0)))
    return padded[:values.shape[0]]

def advanced_rows(values, dilation_offset):
    padded = jnp.pad(values, ((0, dilation_offset), (0, 0)))
    return padded[dilation_offset:]

def gate_parts(tapped, layer_in, tap_weight, now_weight):
    pre = jnp.dot(tapped, tap_weight, preferred_element_type=jnp.float32) + jnp.dot(layer_in, now_weight, preferred_element_type=jnp.float32)
    half_width = pre.shape[1] // 2
    return (jnp.tanh(pre[:, :half_width]), jax.nn.sigmoid(pre[:, half_width:]))

def reference(signal, skip_cot, res_cot, w_tap, w_now, w_res, w_skip):
    number, length, channels = signal.shape
    layers_total = w_tap.shape[0]
    streams = [signal[seq_index] for seq_index in range(number)]
    saved = []
    skip_running_sum = [jnp.zeros((length, w_skip.shape[2]), jnp.float32) for seq_index in range(number)]
    for layer_number in range(layers_total):
        dilation_offset = FIRST_DILATION * 2 ** layer_number
        saved.append(streams)
        new_streams = []
        for seq_index in range(number):
            layer_in = streams[seq_index]
            tapped = delayed_rows(layer_in, dilation_offset)
            tanh_part, sigmoid_part = gate_parts(tapped, layer_in, w_tap[layer_number], w_now[layer_number])
            gated = (tanh_part * sigmoid_part).astype(jnp.bfloat16)
            skip_running_sum[seq_index] = skip_running_sum[seq_index] + jnp.dot(gated, w_skip[layer_number], preferred_element_type=jnp.float32)
            new_streams.append((layer_in.astype(jnp.float32) + jnp.dot(gated, w_res[layer_number], preferred_element_type=jnp.float32)).astype(jnp.bfloat16))
        streams = new_streams
    skip_total = jnp.stack(skip_running_sum).astype(jnp.bfloat16)
    grad_scale = 1.0 / math.sqrt(number * length)
    grads_now = [res_cot[seq_index] for seq_index in range(number)]
    input_layers = [None] * layers_total
    tap_list = [None] * layers_total
    now_list = [None] * layers_total
    res_list = [None] * layers_total
    skip_list = [None] * layers_total
    for layer_number in reversed(range(layers_total)):
        dilation_offset = FIRST_DILATION * 2 ** layer_number
        grad_tap = jnp.zeros(w_tap.shape[1:], jnp.float32)
        grad_now = jnp.zeros(w_now.shape[1:], jnp.float32)
        grad_res = jnp.zeros(w_res.shape[1:], jnp.float32)
        grad_skip = jnp.zeros(w_skip.shape[1:], jnp.float32)
        new_grads = []
        for seq_index in range(number):
            layer_in = saved[layer_number][seq_index]
            grad_out = grads_now[seq_index]
            skip_grad = skip_cot[seq_index]
            tapped = delayed_rows(layer_in, dilation_offset)
            tanh_part, sigmoid_part = gate_parts(tapped, layer_in, w_tap[layer_number], w_now[layer_number])
            gated = (tanh_part * sigmoid_part).astype(jnp.bfloat16)
            grad_gated = jnp.dot(grad_out, w_res[layer_number].T, preferred_element_type=jnp.float32) + jnp.dot(skip_grad, w_skip[layer_number].T, preferred_element_type=jnp.float32)
            grad_pre = jnp.concatenate([grad_gated * sigmoid_part * (1.0 - tanh_part * tanh_part), grad_gated * tanh_part * sigmoid_part * (1.0 - sigmoid_part)], axis=1).astype(jnp.bfloat16)
            grad_tap = grad_tap + jnp.dot(tapped.T, grad_pre, preferred_element_type=jnp.float32)
            grad_now = grad_now + jnp.dot(layer_in.T, grad_pre, preferred_element_type=jnp.float32)
            grad_res = grad_res + jnp.dot(gated.T, grad_out, preferred_element_type=jnp.float32)
            grad_skip = grad_skip + jnp.dot(gated.T, skip_grad, preferred_element_type=jnp.float32)
            back_term = jnp.dot(grad_pre, w_tap[layer_number].T, preferred_element_type=jnp.float32).astype(jnp.bfloat16)
            grad_in = grad_out.astype(jnp.float32) + jnp.dot(grad_pre, w_now[layer_number].T, preferred_element_type=jnp.float32) + advanced_rows(back_term, dilation_offset).astype(jnp.float32)
            new_grads.append(grad_in.astype(jnp.bfloat16))
        grads_now = new_grads
        input_layers[layer_number] = jnp.stack(new_grads)
        tap_list[layer_number] = grad_tap * grad_scale
        now_list[layer_number] = grad_now * grad_scale
        res_list[layer_number] = grad_res * grad_scale
        skip_list[layer_number] = grad_skip * grad_scale
    return (skip_total, jnp.stack(input_layers), jnp.stack(tap_list), jnp.stack(now_list), jnp.stack(res_list), jnp.stack(skip_list))
```

```python
import math

import jax
import jax.numpy as jnp
from jax import lax
from jax.experimental import pallas as pl
from jax.experimental.pallas import tpu as pltpu
from jax.sharding import PartitionSpec as P

MESH = pl.DeviceIdType.MESH
BF = jnp.bfloat16
F32 = jnp.float32

SECTIONS = 4
YS, ZS, CORES = 4, 8, 2
SHARDS = YS * ZS * CORES
SPAN = 4
ROWS, CH = 512, 256
PARTS = 2
PART = ROWS // PARTS
HALF_ROWS = 384
PIECE = HALF_ROWS // ZS
LANES = 128


def dot(a, b):
    return jnp.dot(a, b, preferred_element_type=F32)


def dot_bt(a, b):
    return lax.dot_general(a, b, (((1,), (1,)), ((), ())), preferred_element_type=F32)


def dot_at(a, b):
    return lax.dot_general(a, b, (((0,), (0,)), ((), ())), preferred_element_type=F32)


def kernel(
    signal, skip_cot, res_cot, w_tap, w_now, w_res, w_skip,
    out_skip, out_grads, out_sums,
    wts, th, act, sig, gated_s, skip_acc, skip_out, cot, grad, dz, back_s, back_r, part_g,
    sums, pair_r, pair_s, y_r, y_s, z_r, z_s, x_r, full,
    sem_in, sem_loc, w_ss, w_rs, wp_ss, wp_rs, tap_ss, tap_rs, back_ss, back_rs,
    skip_ss, skip_rs, ig_ss, ig_rs, s1_ss, s1_rs, s2_ss, s2_rs, s3_ss, s3_rs,
    s4_ss, s4_rs, s5_ss, s5_rs, s6_ss, s6_rs, s7_ss, s7_rs,
):
    x = lax.axis_index("section")
    t = lax.axis_index("tm")
    core = lax.rem(t, CORES)
    z = lax.rem(t // CORES, ZS)
    y = t // (CORES * ZS)
    mate = t + 1 - 2 * core

    def at_x(j):
        return lax.rem(x + j + SECTIONS, SECTIONS)

    def at_y(j):
        return (lax.rem(y + j + YS, YS) * ZS + z) * CORES + core

    def at_z(j):
        return (y * ZS + lax.rem(z + j + ZS, ZS)) * CORES + core

    def rows(c):
        return pl.ds(c * PART, PART)

    def remote(src, dst, ss, rs, to_x, to_t):
        return pltpu.make_async_remote_copy(
            src_ref=src, dst_ref=dst, send_sem=ss, recv_sem=rs,
            device_id=(to_x, to_t), device_id_type=MESH,
        )

    def w_copy(layer, j):
        half = pl.ds(core * HALF_ROWS, HALF_ROWS)
        return remote(
            wts.at[layer, half], wts.at[layer, half],
            w_ss.at[j - 1], w_rs.at[j - 1], at_x(j), t,
        )

    def w_recv(layer):
        j = lax.rem(x - layer + SECTIONS, SECTIONS)
        half = pl.ds(core * HALF_ROWS, HALF_ROWS)
        return remote(
            wts.at[layer, half], wts.at[layer, half],
            w_ss.at[j - 1], w_rs.at[j - 1], layer, t,
        )

    def w_mate(layer, whose):
        half = pl.ds(whose * HALF_ROWS, HALF_ROWS)
        return remote(
            wts.at[layer, half], wts.at[layer, half],
            wp_ss.at[layer], wp_rs.at[layer], x, mate,
        )

    def tap_copy(layer, c, to_t):
        return remote(
            th.at[layer, rows(c), pl.ds(CH, CH)], th.at[layer, rows(c), pl.ds(0, CH)],
            tap_ss.at[layer * PARTS + c], tap_rs.at[layer * PARTS + c], x, to_t,
        )

    def tap_first(c, to_t):
        return remote(
            signal.at[x, rows(c)], th.at[0, rows(c), pl.ds(0, CH)],
            tap_ss.at[c], tap_rs.at[c], x, to_t,
        )

    def back_copy(layer, c, to_t):
        return remote(
            back_s.at[layer, rows(c)], back_r.at[layer, rows(c)],
            back_ss.at[layer * PARTS + c], back_rs.at[layer * PARTS + c], x, to_t,
        )

    def skip_copy(j):
        return remote(
            skip_out, out_skip.at[x], skip_ss.at[j - 1], skip_rs.at[j - 1], at_x(j), t
        )

    def skip_recv(j):
        return remote(
            skip_out, out_skip.at[at_x(-j)], skip_ss.at[j - 1], skip_rs.at[j - 1], at_x(-j), t
        )

    def ig_copy(layer, c):
        j = lax.rem(layer - x + SECTIONS, SECTIONS)
        return remote(
            grad.at[layer, rows(c)], out_grads.at[0, x, rows(c)],
            ig_ss.at[layer * PARTS + c], ig_rs.at[(j - 1) * PARTS + c], layer, t,
        )

    def ig_recv(j, c):
        return remote(
            grad.at[0, rows(c)], out_grads.at[0, at_x(-j), rows(c)],
            ig_ss.at[c], ig_rs.at[(j - 1) * PARTS + c], at_x(-j), t,
        )

    def ig_own(layer, c):
        return pltpu.make_async_copy(
            grad.at[layer, rows(c)], out_grads.at[0, x, rows(c)], sem_loc.at[c]
        )

    def s1(layer):
        return remote(
            sums.at[layer, 1 - core], pair_r.at[layer],
            s1_ss.at[layer], s1_rs.at[layer], x, mate,
        )

    def s2(layer, j):
        return remote(
            pair_s.at[layer, lax.rem(y + j, YS)], y_r.at[layer, j - 1],
            s2_ss.at[layer * 3 + j - 1], s2_rs.at[layer * 3 + j - 1], x, at_y(j),
        )

    def piece(i):
        return pl.ds(pl.multiple_of(i * PIECE, 16), PIECE)

    def s3(layer, j):
        return remote(
            y_s.at[layer, piece(lax.rem(z + j, ZS))], z_r.at[layer, j - 1],
            s3_ss.at[layer * 7 + j - 1], s3_rs.at[layer * 7 + j - 1], x, at_z(j),
        )

    def s4(layer):
        j = lax.rem(layer - x + SECTIONS, SECTIONS)
        return remote(
            z_s.at[layer], x_r.at[j - 1], s4_ss.at[layer], s4_rs.at[j - 1], layer, t
        )

    def s4_recv(j):
        return remote(z_s.at[0], x_r.at[j - 1], s4_ss.at[0], s4_rs.at[j - 1], at_x(-j), t)

    def s5(j, whose):
        return remote(
            full.at[core, y, piece(whose)], full.at[core, y, piece(whose)],
            s5_ss.at[j - 1], s5_rs.at[j - 1], x, at_z(j),
        )

    def s6(j, whose):
        return remote(
            full.at[core, whose], full.at[core, whose],
            s6_ss.at[j - 1], s6_rs.at[j - 1], x, at_y(j),
        )

    def s7(whose):
        return remote(full.at[whose], full.at[whose], s7_ss.at[0], s7_rs.at[0], x, mate)

    loads = [
        pltpu.make_async_copy(w_tap.at[0], wts.at[x, pl.ds(0, CH)], sem_in.at[0]),
        pltpu.make_async_copy(w_now.at[0], wts.at[x, pl.ds(CH, CH)], sem_in.at[1]),
        pltpu.make_async_copy(
            w_res.at[0], wts.at[x, pl.ds(2 * CH, CH), pl.ds(0, CH)], sem_in.at[2]
        ),
        pltpu.make_async_copy(
            w_skip.at[0], wts.at[x, pl.ds(2 * CH, CH), pl.ds(CH, CH)], sem_in.at[3]
        ),
        pltpu.make_async_copy(signal.at[x], th.at[0, :, pl.ds(CH, CH)], sem_in.at[4]),
        pltpu.make_async_copy(skip_cot.at[x], cot, sem_in.at[5]),
        pltpu.make_async_copy(res_cot.at[x], grad.at[SECTIONS], sem_in.at[6]),
    ]
    for load in loads:
        load.start()

    barrier = pltpu.get_barrier_semaphore()
    peers = [(at_x(j), t) for j in range(1, SECTIONS)] + [(x, mate)]
    peers += [(x, at_y(j)) for j in range(1, YS)] + [(x, at_z(j)) for j in range(1, ZS)]
    peers += [(x, lax.rem(t + d + SHARDS, SHARDS)) for d in (SPAN, -SPAN, 2 * SPAN, -2 * SPAN)]
    for peer in peers:
        pl.semaphore_signal(barrier, inc=1, device_id=peer, device_id_type=MESH)
    pl.semaphore_wait(barrier, len(peers))

    @pl.when(t + SPAN < SHARDS)
    def _():
        for c in range(PARTS):
            tap_first(c, t + SPAN).start()

    for load in loads[:4]:
        load.wait()
    for j in range(1, SECTIONS):
        w_copy(x, j).start()

    for layer in range(SECTIONS):
        d = SPAN << layer

        @pl.when(t < d)
        def _(layer=layer):
            th[layer, :, pl.ds(0, CH)] = jnp.zeros((ROWS, CH), BF)

        @pl.when(t + d >= SHARDS)
        def _(layer=layer):
            back_r[layer] = jnp.zeros((ROWS, CH), BF)

    skip_acc[...] = jnp.zeros((ROWS, CH), F32)
    for load in loads[4:]:
        load.wait()

    def w_forward(layer):
        @pl.when(x != layer)
        def _():
            w_recv(layer).wait_recv()
            w_mate(layer, core).start()

    w_forward(0)

    def forward(k, d):
        @pl.when(x != k)
        def _():
            w_mate(k, 1 - core).wait_recv()

        for c in range(PARTS):
            @pl.when(t >= d)
            def _():
                tap_copy(k, c, t).wait_recv()

            pre = dot(th[k, rows(c), :], wts[k, pl.ds(0, 2 * CH), :])
            a = jnp.tanh(pre[:, :CH])
            s = jax.nn.sigmoid(pre[:, CH:])
            act[k, rows(c), :] = a
            sig[k, rows(c), :] = s
            gated = (a * s).astype(BF)
            gated_s[k, rows(c), :] = gated
            out = dot(gated, wts[k, pl.ds(2 * CH, CH), :])
            skip_acc[rows(c), :] += out[:, CH:]
            h = th[k, rows(c), pl.ds(CH, CH)].astype(F32)
            th[k + 1, rows(c), pl.ds(CH, CH)] = (h + out[:, :CH]).astype(BF)

            @pl.when(jnp.logical_and(k < SECTIONS - 1, t + 2 * d < SHARDS))
            def _():
                tap_copy(k + 1, c, t + 2 * d).start()

        @pl.when(k < SECTIONS - 1)
        def _():
            w_forward(k + 1)

        return d * 2

    lax.fori_loop(0, SECTIONS, forward, jnp.int32(SPAN))

    skip_out[...] = skip_acc[...].astype(BF)
    for j in range(1, SECTIONS):
        skip_copy(j).start()
    skip_own = pltpu.make_async_copy(skip_out, out_skip.at[x], sem_loc.at[2])
    skip_own.start()

    def s1_to_s2(layer):
        s1(layer).wait_recv()
        pair_s[layer] = (
            sums[layer, core].astype(F32) + pair_r[layer].astype(F32)
        ).astype(BF)
        for j in range(1, YS):
            s2(layer, j).start()

    def s2_to_s3(layer):
        total = pair_s[layer, y].astype(F32)
        for j in range(1, YS):
            s2(layer, j).wait_recv()
            total = total + y_r[layer, j - 1].astype(F32)
        y_s[layer] = total.astype(BF)
        for j in range(1, ZS):
            s3(layer, j).start()

    def s3_to_s4(layer):
        total = y_s[layer, piece(z), :].astype(F32)
        for j in range(1, ZS):
            s3(layer, j).wait_recv()
            total = total + z_r[layer, j - 1].astype(F32)
        z_s[layer] = total.astype(BF)

        @pl.when(x != layer)
        def _():
            s4(layer).start()

    def finish_grad(layer, d, c):
        @pl.when(t + d < SHARDS)
        def _():
            back_copy(layer, c, t).wait_recv()

        g = (part_g[rows(c), :] + back_r[layer, rows(c), :].astype(F32)).astype(BF)
        grad[layer, rows(c), :] = g

        @pl.when(x != layer)
        def _():
            ig_copy(layer, c).start()

        @pl.when(x == layer)
        def _():
            ig_own(layer, c).start()

    def backward(i, d):
        k = SECTIONS - 1 - i
        for c in range(PARTS):
            @pl.when(i > 0)
            def _():
                finish_grad(k + 1, 2 * d, c)

            g = grad[k + 1, rows(c), :]
            du = dot_bt(g, wts[k, pl.ds(2 * CH, CH), pl.ds(0, CH)]) + dot_bt(
                cot[rows(c), :], wts[k, pl.ds(2 * CH, CH), pl.ds(CH, CH)]
            )
            a = act[k, rows(c), :]
            s = sig[k, rows(c), :]
            us = du * s
            dz[rows(c), pl.ds(0, CH)] = (us * (1.0 - a * a)).astype(BF)
            dz[rows(c), pl.ds(CH, CH)] = (us * a * (1.0 - s)).astype(BF)
            both = dot_bt(dz[rows(c), :], wts[k, pl.ds(0, 2 * CH), :])
            back_s[k, rows(c), :] = both[:, :CH].astype(BF)

            @pl.when(t >= d)
            def _():
                back_copy(k, c, t - d).start()

            part_g[rows(c), :] = g.astype(F32) + both[:, CH:]

        for n in range(2):
            cols = pl.ds(n * CH, CH)
            first = dot_at(th[k], dz[:, cols]).astype(BF)
            right = grad[k + 1] if n == 0 else cot[...]
            second = dot_at(gated_s[k], right).astype(BF)
            for m in range(2):
                block = 2 * n + m
                lanes = slice(m * LANES, (m + 1) * LANES)
                sums[k, 0, block] = first[:HALF_ROWS, lanes]
                sums[k, 1, block, pl.ds(0, 2 * CH - HALF_ROWS), :] = first[HALF_ROWS:, lanes]
                sums[k, 1, block, pl.ds(2 * CH - HALF_ROWS, CH), :] = second[:, lanes]
        s1(k).start()

        @pl.when(i >= 1)
        def _():
            s1_to_s2(k + 1)

        @pl.when(i >= 2)
        def _():
            s2_to_s3(k + 2)

        @pl.when(i >= 3)
        def _():
            s3_to_s4(k + 3)

        return d // 2

    lax.fori_loop(0, SECTIONS, backward, jnp.int32(SPAN << (SECTIONS - 1)))

    s1_to_s2(0)
    s2_to_s3(1)
    s3_to_s4(2)
    finish_grad(0, SPAN, 0)
    s2_to_s3(0)
    s3_to_s4(1)
    finish_grad(0, SPAN, 1)
    s3_to_s4(0)

    total = z_s[x].astype(F32)
    for j in range(1, SECTIONS):
        s4_recv(j).wait_recv()
        total = total + x_r[j - 1].astype(F32)
    full[core, y, piece(z), :] = total.astype(BF)
    for j in range(1, ZS):
        s5(j, z).start()
    for j in range(1, ZS):
        s5(j, lax.rem(z - j + ZS, ZS)).wait_recv()
    for j in range(1, YS):
        s6(j, y).start()
    for j in range(1, YS):
        s6(j, lax.rem(y - j + YS, YS)).wait_recv()
    s7(core).start()
    s7(1 - core).wait_recv()
    done = pltpu.make_async_copy(full, out_sums, sem_loc.at[3])
    done.start()

    for j in range(1, SECTIONS):
        w_copy(x, j).wait_send()
        skip_copy(j).wait_send()
        skip_recv(j).wait_recv()
        for c in range(PARTS):
            ig_recv(j, c).wait_recv()
    skip_own.wait()
    for c in range(PARTS):
        ig_own(x, c).wait()
    for j in range(1, ZS):
        s5(j, z).wait_send()
    for j in range(1, YS):
        s6(j, y).wait_send()
    s7(core).wait_send()

    def drain(k, d):
        @pl.when(x != k)
        def _():
            w_mate(k, core).wait_send()
            s4(k).wait_send()
            for c in range(PARTS):
                ig_copy(k, c).wait_send()

        for c in range(PARTS):
            @pl.when(t + d < SHARDS)
            def _():
                tap_copy(k, c, t).wait_send()

            @pl.when(t >= d)
            def _():
                back_copy(k, c, t).wait_send()

        s1(k).wait_send()
        for j in range(1, YS):
            s2(k, j).wait_send()
        for j in range(1, ZS):
            s3(k, j).wait_send()
        return d * 2

    lax.fori_loop(0, SECTIONS, drain, jnp.int32(SPAN))
    done.wait()


def body(signal, skip_cot, res_cot, w_tap, w_now, w_res, w_skip):
    any_space = pl.BlockSpec(memory_space=pl.ANY)
    dma = pltpu.SemaphoreType.DMA
    n = SECTIONS
    skip_total, input_grads, sums = pl.pallas_call(
        kernel,
        out_shape=(
            jax.ShapeDtypeStruct((n, ROWS, CH), BF),
            jax.ShapeDtypeStruct((1, n, ROWS, CH), BF),
            jax.ShapeDtypeStruct((CORES, YS, HALF_ROWS, LANES), BF),
        ),
        in_specs=[any_space] * 7,
        out_specs=(any_space,) * 3,
        scratch_shapes=[
            pltpu.VMEM((n, 3 * CH, 2 * CH), BF),
            pltpu.VMEM((n + 1, ROWS, 2 * CH), BF),
            pltpu.VMEM((n, ROWS, CH), F32),
            pltpu.VMEM((n, ROWS, CH), F32),
            pltpu.VMEM((n, ROWS, CH), BF),
            pltpu.VMEM((ROWS, CH), F32),
            pltpu.VMEM((ROWS, CH), BF),
            pltpu.VMEM((ROWS, CH), BF),
            pltpu.VMEM((n + 1, ROWS, CH), BF),
            pltpu.VMEM((ROWS, 2 * CH), BF),
            pltpu.VMEM((n, ROWS, CH), BF),
            pltpu.VMEM((n, ROWS, CH), BF),
            pltpu.VMEM((ROWS, CH), F32),
            pltpu.VMEM((n, CORES, YS, HALF_ROWS, LANES), BF),
            pltpu.VMEM((n, YS, HALF_ROWS, LANES), BF),
            pltpu.VMEM((n, YS, HALF_ROWS, LANES), BF),
            pltpu.VMEM((n, YS - 1, HALF_ROWS, LANES), BF),
            pltpu.VMEM((n, HALF_ROWS, LANES), BF),
            pltpu.VMEM((n, ZS - 1, PIECE, LANES), BF),
            pltpu.VMEM((n, PIECE, LANES), BF),
            pltpu.VMEM((n - 1, PIECE, LANES), BF),
            pltpu.VMEM((CORES, YS, HALF_ROWS, LANES), BF),
            dma((7,)),
            dma((4,)),
            dma((n - 1,)), dma((n - 1,)),
            dma((n,)), dma((n,)),
            dma((n * PARTS,)), dma((n * PARTS,)),
            dma((n * PARTS,)), dma((n * PARTS,)),
            dma((n - 1,)), dma((n - 1,)),
            dma((n * PARTS,)), dma(((n - 1) * PARTS,)),
            dma((n,)), dma((n,)),
            dma((n * (YS - 1),)), dma((n * (YS - 1),)),
            dma((n * (ZS - 1),)), dma((n * (ZS - 1),)),
            dma((n,)), dma((n - 1,)),
            dma((ZS - 1,)), dma((ZS - 1,)),
            dma((YS - 1,)), dma((YS - 1,)),
            dma((1,)), dma((1,)),
        ],
        compiler_params=pltpu.CompilerParams(
            collective_id=0, has_side_effects=True, vmem_limit_bytes=56 << 20
        ),
    )(signal, skip_cot, res_cot, w_tap, w_now, w_res, w_skip)
    scale = 1.0 / math.sqrt(n * ROWS * SHARDS)
    packed = sums.astype(F32) * scale
    packed = packed.transpose(0, 2, 1, 3).reshape(1, 3 * CH, 2 * CH)
    return (
        skip_total,
        input_grads,
        packed[:, :CH],
        packed[:, CH : 2 * CH],
        packed[:, 2 * CH :, :CH],
        packed[:, 2 * CH :, CH:],
    )


def solution(mesh):
    rows3 = P(None, "tm", None)
    owned = P("section", None, None)
    return jax.shard_map(
        body,
        mesh=mesh,
        in_specs=(rows3,) * 3 + (owned,) * 4,
        out_specs=(rows3, P("section", None, "tm", None)) + (owned,) * 4,
        check_vma=False,
    )
```

```python
import math

import jax
import jax.numpy as jnp
from jax import lax
from jax.experimental import pallas as pl
from jax.experimental.pallas import tpu as pltpu
from jax.sharding import PartitionSpec as P

MESH = pl.DeviceIdType.MESH
BF = jnp.bfloat16
F32 = jnp.float32

SECTIONS = 4
YS, ZS, CORES = 4, 8, 2
SHARDS = YS * ZS * CORES
ROWS, CH = 512, 256
GROUP = 16
BLOCK = ROWS // GROUP
LEAD = ROWS // 2
PARTS = 2
PART = ROWS // PARTS
HALF_ROWS = 384
PIECE = HALF_ROWS // ZS
LANES = 128


def dot(a, b):
    return jnp.dot(a, b, preferred_element_type=F32)


def dot_bt(a, b):
    return lax.dot_general(a, b, (((1,), (1,)), ((), ())), preferred_element_type=F32)


def dot_at(a, b):
    return lax.dot_general(a, b, (((0,), (0,)), ((), ())), preferred_element_type=F32)


def kernel(
    signal, skip_cot, res_cot, w_tap, w_now, w_res, w_skip,
    out_skip, out_grads, out_tap, out_now, out_res, out_wskip,
    wts, hp, act, sig, gated_s, skip_acc, skip_out, skip_t, cot, grad, dz, bp, part_g,
    sums, pair_r, pair_s, y_r, y_s, z_r, z_s, x_r, full,
    sem_in, sem_loc, w_ss, w_rs, wp_ss, wp_rs, in_ss, in_rs,
    skt_ss, skt_rs, skip_ss, skip_rs, ig_ss, ig_rs, s1_ss, s1_rs, s2_ss, s2_rs, s3_ss, s3_rs,
    s4_ss, s4_rs, s5_ss, s5_rs, s6_ss, s6_rs, s7_ss, s7_rs,
):
    x = lax.axis_index("section")
    t = lax.axis_index("tm")
    core = lax.rem(t, CORES)
    z = lax.rem(t // CORES, ZS)
    y = t // (CORES * ZS)
    z_half, z_odd = z // 2, lax.rem(z, 2)
    me = y * 4 + z_half
    mate = t + 1 - 2 * core

    def at_x(j):
        return lax.rem(x + j + SECTIONS, SECTIONS)

    def at_y(j):
        return (lax.rem(y + j + YS, YS) * ZS + z) * CORES + core

    def at_z(j):
        return (y * ZS + lax.rem(z + j + ZS, ZS)) * CORES + core

    def member(j):
        dy, dz = j // 4, j % 4
        py, pz = lax.rem(y + dy, YS), lax.rem(z_half + dz, 4)
        return py * 4 + pz, (py * ZS + pz * 2 + z_odd) * CORES + core

    def rows(c):
        return pl.ds(c * PART, PART)

    def block(i, lead=0):
        return pl.ds(pl.multiple_of(lead + i * BLOCK, BLOCK), BLOCK)

    def remote(src, dst, ss, rs, to_x, to_t):
        return pltpu.make_async_remote_copy(
            src_ref=src, dst_ref=dst, send_sem=ss, recv_sem=rs,
            device_id=(to_x, to_t), device_id_type=MESH,
        )

    def w_copy(layer, j):
        half = pl.ds(core * HALF_ROWS, HALF_ROWS)
        return remote(
            wts.at[layer, half], wts.at[layer, half],
            w_ss.at[j - 1], w_rs.at[j - 1], at_x(j), t,
        )

    def w_recv(layer):
        j = lax.rem(x - layer + SECTIONS, SECTIONS)
        half = pl.ds(core * HALF_ROWS, HALF_ROWS)
        return remote(
            wts.at[layer, half], wts.at[layer, half],
            w_ss.at[j - 1], w_rs.at[j - 1], layer, t,
        )

    def w_mate(layer, whose):
        half = pl.ds(whose * HALF_ROWS, HALF_ROWS)
        return remote(
            wts.at[layer, half], wts.at[layer, half],
            wp_ss.at[layer], wp_rs.at[layer], x, mate,
        )

    inputs = (signal, skip_cot, res_cot)
    places = ((hp.at[0], LEAD), (cot, 0), (grad.at[SECTIONS], 0))

    def spread(n, j):
        place, shard = member(j)
        to, lead = places[n]
        return remote(
            inputs[n].at[x, block(place)], to.at[block(me, lead)],
            in_ss.at[n], in_rs.at[n], x, shard,
        )

    def spread_own(n):
        to, lead = places[n]
        return pltpu.make_async_copy(
            inputs[n].at[x, block(me)], to.at[block(me, lead)], sem_in.at[4 + n]
        )

    def others(ss, rs):
        some = cot.at[pl.ds(0, ROWS - BLOCK)]
        return remote(some, some, ss, rs, x, mate)

    def whole(ss, rs):
        return remote(cot, cot, ss, rs, x, mate)

    def skip_back(j):
        place, shard = member(j)
        return remote(
            skip_out.at[block(place)], skip_t.at[block(me)], skt_ss.at[0], skt_rs.at[0], x, shard
        )

    def skip_copy(j):
        return remote(
            skip_t, out_skip.at[x], skip_ss.at[j - 1], skip_rs.at[j - 1], at_x(j), t
        )

    def skip_recv(j):
        return remote(
            skip_t, out_skip.at[at_x(-j)], skip_ss.at[j - 1], skip_rs.at[j - 1], at_x(-j), t
        )

    def ig_copy(layer, j):
        place, shard = member(j)
        return remote(
            grad.at[layer, block(place)], out_grads.at[0, x, block(me)],
            ig_ss.at[layer], ig_rs.at[lax.rem(layer - x + SECTIONS, SECTIONS)], layer, shard,
        )

    def ig_own(layer):
        return pltpu.make_async_copy(
            grad.at[layer, block(me)], out_grads.at[0, x, block(me)], sem_loc.at[0]
        )

    def s1(layer):
        return remote(
            sums.at[layer, 1 - core], pair_r.at[layer],
            s1_ss.at[layer], s1_rs.at[layer], x, mate,
        )

    def s2(layer, j):
        return remote(
            pair_s.at[layer, lax.rem(y + j, YS)], y_r.at[layer, j - 1],
            s2_ss.at[layer * 3 + j - 1], s2_rs.at[layer * 3 + j - 1], x, at_y(j),
        )

    def piece(i):
        return pl.ds(pl.multiple_of(i * PIECE, 16), PIECE)

    def s3(layer, j):
        return remote(
            y_s.at[layer, piece(lax.rem(z + j, ZS))], z_r.at[layer, j - 1],
            s3_ss.at[layer * 7 + j - 1], s3_rs.at[layer * 7 + j - 1], x, at_z(j),
        )

    def s4(layer):
        j = lax.rem(layer - x + SECTIONS, SECTIONS)
        return remote(
            z_s.at[layer], x_r.at[j - 1], s4_ss.at[layer], s4_rs.at[j - 1], layer, t
        )

    def s4_recv(j):
        return remote(z_s.at[0], x_r.at[j - 1], s4_ss.at[0], s4_rs.at[j - 1], at_x(-j), t)

    def s5(j, whose):
        return remote(
            full.at[core, y, piece(whose)], full.at[core, y, piece(whose)],
            s5_ss.at[j - 1], s5_rs.at[j - 1], x, at_z(j),
        )

    def s6(j, whose):
        return remote(
            full.at[core, whose], full.at[core, whose],
            s6_ss.at[j - 1], s6_rs.at[j - 1], x, at_y(j),
        )

    def s7(whose):
        return remote(full.at[whose], full.at[whose], s7_ss.at[0], s7_rs.at[0], x, mate)

    loads = [
        pltpu.make_async_copy(w_tap.at[0], wts.at[x, pl.ds(0, CH)], sem_in.at[0]),
        pltpu.make_async_copy(w_now.at[0], wts.at[x, pl.ds(CH, CH)], sem_in.at[1]),
        pltpu.make_async_copy(
            w_res.at[0], wts.at[x, pl.ds(2 * CH, CH), pl.ds(0, CH)], sem_in.at[2]
        ),
        pltpu.make_async_copy(
            w_skip.at[0], wts.at[x, pl.ds(2 * CH, CH), pl.ds(CH, CH)], sem_in.at[3]
        ),
    ] + [spread_own(n) for n in range(3)]
    for load in loads:
        load.start()

    barrier = pltpu.get_barrier_semaphore()
    peers = [(x, mate)] + [(x, at_z(j)) for j in (1, 3, 5, 7)]
    peers += [(x, member(j)[1]) for j in range(1, GROUP)]
    peers += [(at_x(i), member(j)[1]) for i in range(1, SECTIONS) for j in range(GROUP)]
    for peer in peers:
        pl.semaphore_signal(barrier, inc=1, device_id=peer, device_id_type=MESH)

    for layer in range(SECTIONS):
        hp[layer, pl.ds(0, LEAD), :] = jnp.zeros((LEAD, CH), BF)
    bp[pl.ds(ROWS, LEAD), :] = jnp.zeros((LEAD, CH), BF)
    skip_acc[...] = jnp.zeros((ROWS, CH), F32)
    pl.semaphore_wait(barrier, len(peers))

    for j in range(1, GROUP):
        spread(0, j).start()
    for load in loads[:4]:
        load.wait()
    for j in range(1, SECTIONS):
        w_copy(x, j).start()
    for n in (1, 2):
        for j in range(1, GROUP):
            spread(n, j).start()

    def w_forward(layer):
        @pl.when(x != layer)
        def _():
            w_recv(layer).wait_recv()
            w_mate(layer, core).start()

    for layer in range(SECTIONS):
        w_forward(layer)
    loads[4].wait()
    others(in_ss.at[0], in_rs.at[0]).wait_recv()

    def tap_rows(c, shift):
        return pl.ds(pl.multiple_of(LEAD + c * PART - shift, BLOCK), PART)

    def forward(k, shift):
        @pl.when(x != k)
        def _():
            w_mate(k, 1 - core).wait_recv()

        for c in range(PARTS):
            here = pl.ds(LEAD + c * PART, PART)
            h = hp[k, here, :]
            pre = dot(hp[k, tap_rows(c, shift), :], wts[k, pl.ds(0, CH), :]) + dot(
                h, wts[k, pl.ds(CH, CH), :]
            )
            a = jnp.tanh(pre[:, :CH])
            s = jax.nn.sigmoid(pre[:, CH:])
            act[k, rows(c), :] = a
            sig[k, rows(c), :] = s
            gated = (a * s).astype(BF)
            gated_s[k, rows(c), :] = gated
            out = dot(gated, wts[k, pl.ds(2 * CH, CH), :])
            skip_acc[rows(c), :] += out[:, CH:]
            hp[k + 1, here, :] = (h.astype(F32) + out[:, :CH]).astype(BF)

        return shift * 2

    lax.fori_loop(0, SECTIONS, forward, jnp.int32(BLOCK))

    skip_out[...] = skip_acc[...].astype(BF)
    for j in range(1, GROUP):
        skip_back(j).start()
    skip_mine = pltpu.make_async_copy(
        skip_out.at[block(me)], skip_t.at[block(me)], sem_loc.at[1]
    )
    skip_mine.start()

    def s1_to_s2(layer):
        s1(layer).wait_recv()
        pair_s[layer] = (
            sums[layer, core].astype(F32) + pair_r[layer].astype(F32)
        ).astype(BF)
        for j in range(1, YS):
            s2(layer, j).start()

    def s2_to_s3(layer):
        total = pair_s[layer, y].astype(F32)
        for j in range(1, YS):
            s2(layer, j).wait_recv()
            total = total + y_r[layer, j - 1].astype(F32)
        y_s[layer] = total.astype(BF)
        for j in range(1, ZS):
            s3(layer, j).start()

    def s3_to_s4(layer):
        total = y_s[layer, piece(z), :].astype(F32)
        for j in range(1, ZS):
            s3(layer, j).wait_recv()
            total = total + z_r[layer, j - 1].astype(F32)
        z_s[layer] = total.astype(BF)

        @pl.when(x != layer)
        def _():
            s4(layer).start()

    for n in (1, 2):
        loads[4 + n].wait()
        others(in_ss.at[n], in_rs.at[n]).wait_recv()

    def backward(i, shift):
        k = SECTIONS - 1 - i
        for c in range(PARTS):
            g = grad[k + 1, rows(c), :]
            du = dot_bt(g, wts[k, pl.ds(2 * CH, CH), pl.ds(0, CH)]) + dot_bt(
                cot[rows(c), :], wts[k, pl.ds(2 * CH, CH), pl.ds(CH, CH)]
            )
            a = act[k, rows(c), :]
            s = sig[k, rows(c), :]
            us = du * s
            dz[rows(c), pl.ds(0, CH)] = (us * (1.0 - a * a)).astype(BF)
            dz[rows(c), pl.ds(CH, CH)] = (us * a * (1.0 - s)).astype(BF)
            both = dot_bt(dz[rows(c), :], wts[k, pl.ds(0, 2 * CH), :])
            bp[rows(c), :] = both[:, :CH].astype(BF)
            part_g[rows(c), :] = g.astype(F32) + both[:, CH:]

        for c in range(PARTS):
            later = pl.ds(pl.multiple_of(c * PART + shift, BLOCK), PART)
            grad[k, rows(c), :] = (part_g[rows(c), :] + bp[later, :].astype(F32)).astype(BF)

        for n in range(2):
            cols = pl.ds(n * CH, CH)
            right = dz[:, cols]
            tap = hp[k, pl.ds(pl.multiple_of(LEAD - shift, BLOCK), ROWS), :]
            tap_sum = dot_at(tap, right).astype(BF)
            now_sum = dot_at(hp[k, pl.ds(LEAD, ROWS), :], right).astype(BF)
            out_sum = dot_at(gated_s[k], grad[k + 1] if n == 0 else cot[...]).astype(BF)
            rest = HALF_ROWS - CH
            for m in range(2):
                at = 2 * n + m
                lanes = slice(m * LANES, (m + 1) * LANES)
                sums[k, 0, at, pl.ds(0, CH), :] = tap_sum[:, lanes]
                sums[k, 0, at, pl.ds(CH, rest), :] = now_sum[:rest, lanes]
                sums[k, 1, at, pl.ds(0, CH - rest), :] = now_sum[rest:, lanes]
                sums[k, 1, at, pl.ds(CH - rest, CH), :] = out_sum[:, lanes]
        s1(k).start()

        @pl.when(x != k)
        def _():
            ig_copy(k, 0).start()

        @pl.when(x == k)
        def _():
            ig_own(k).start()

        for j in range(1, GROUP):
            ig_copy(k, j).start()

        @pl.when(i >= 1)
        def _():
            s1_to_s2(k + 1)

        return shift // 2

    lax.fori_loop(0, SECTIONS, backward, jnp.int32(BLOCK << (SECTIONS - 1)))

    s1_to_s2(0)
    skip_mine.wait()
    others(skt_ss.at[0], skt_rs.at[0]).wait_recv()
    for j in range(1, SECTIONS):
        skip_copy(j).start()
    skip_own = pltpu.make_async_copy(skip_t, out_skip.at[x], sem_loc.at[2])
    skip_own.start()
    s2_to_s3(3)
    s2_to_s3(2)
    s3_to_s4(3)
    s2_to_s3(1)
    s3_to_s4(2)
    s2_to_s3(0)
    s3_to_s4(1)
    s3_to_s4(0)

    total = z_s[x].astype(F32)
    for j in range(1, SECTIONS):
        s4_recv(j).wait_recv()
        total = total + x_r[j - 1].astype(F32)
    full[core, y, piece(z), :] = total.astype(BF)
    for j in range(1, ZS):
        s5(j, z).start()
    for j in range(1, ZS):
        s5(j, lax.rem(z - j + ZS, ZS)).wait_recv()
    for j in range(1, YS):
        s6(j, y).start()
    for j in range(1, YS):
        s6(j, lax.rem(y - j + YS, YS)).wait_recv()
    s7(core).start()
    s7(1 - core).wait_recv()
    scale = 1.0 / math.sqrt(SECTIONS * ROWS * SHARDS)
    rest = HALF_ROWS - CH
    for at in range(YS):
        lanes = pl.ds(at * LANES, LANES)
        out_tap[0, :, lanes] = full[0, at, pl.ds(0, CH), :].astype(F32) * scale
        out_now[0, pl.ds(0, rest), lanes] = full[0, at, pl.ds(CH, rest), :].astype(F32) * scale
        out_now[0, pl.ds(rest, CH - rest), lanes] = (
            full[1, at, pl.ds(0, CH - rest), :].astype(F32) * scale
        )
        out = out_res if at < 2 else out_wskip
        lanes = pl.ds(at % 2 * LANES, LANES)
        out[0, :, lanes] = full[1, at, pl.ds(CH - rest, CH), :].astype(F32) * scale

    for n in range(3):
        others(in_ss.at[n], in_rs.at[n]).wait_send()
    others(skt_ss.at[0], skt_rs.at[0]).wait_send()
    others(ig_ss.at[x], ig_rs.at[0]).wait_recv()
    others(ig_ss.at[x], ig_rs.at[0]).wait_send()
    for j in range(1, SECTIONS):
        w_copy(x, j).wait_send()
        skip_copy(j).wait_send()
        skip_recv(j).wait_recv()
        whole(ig_ss.at[0], ig_rs.at[j]).wait_recv()
    skip_own.wait()
    ig_own(x).wait()
    for j in range(1, ZS):
        s5(j, z).wait_send()
    for j in range(1, YS):
        s6(j, y).wait_send()
    s7(core).wait_send()

    def drain(k, carry):
        @pl.when(x != k)
        def _():
            w_mate(k, core).wait_send()
            s4(k).wait_send()
            whole(ig_ss.at[k], ig_rs.at[0]).wait_send()

        s1(k).wait_send()
        for j in range(1, YS):
            s2(k, j).wait_send()
        for j in range(1, ZS):
            s3(k, j).wait_send()
        return carry

    lax.fori_loop(0, SECTIONS, drain, jnp.int32(0))


def body(signal, skip_cot, res_cot, w_tap, w_now, w_res, w_skip):
    any_space = pl.BlockSpec(memory_space=pl.ANY)
    vmem = pl.BlockSpec(memory_space=pltpu.VMEM)
    dma = pltpu.SemaphoreType.DMA
    n = SECTIONS
    return pl.pallas_call(
        kernel,
        out_shape=(
            jax.ShapeDtypeStruct((n, ROWS, CH), BF),
            jax.ShapeDtypeStruct((1, n, ROWS, CH), BF),
            jax.ShapeDtypeStruct((1, CH, 2 * CH), F32),
            jax.ShapeDtypeStruct((1, CH, 2 * CH), F32),
            jax.ShapeDtypeStruct((1, CH, CH), F32),
            jax.ShapeDtypeStruct((1, CH, CH), F32),
        ),
        in_specs=[any_space] * 7,
        out_specs=(any_space,) * 2 + (vmem,) * 4,
        scratch_shapes=[
            pltpu.VMEM((n, 3 * CH, 2 * CH), BF),
            pltpu.VMEM((n + 1, LEAD + ROWS, CH), BF),
            pltpu.VMEM((n, ROWS, CH), F32),
            pltpu.VMEM((n, ROWS, CH), F32),
            pltpu.VMEM((n, ROWS, CH), BF),
            pltpu.VMEM((ROWS, CH), F32),
            pltpu.VMEM((ROWS, CH), BF),
            pltpu.VMEM((ROWS, CH), BF),
            pltpu.VMEM((ROWS, CH), BF),
            pltpu.VMEM((n + 1, ROWS, CH), BF),
            pltpu.VMEM((ROWS, 2 * CH), BF),
            pltpu.VMEM((ROWS + LEAD, CH), BF),
            pltpu.VMEM((ROWS, CH), F32),
            pltpu.VMEM((n, CORES, YS, HALF_ROWS, LANES), BF),
            pltpu.VMEM((n, YS, HALF_ROWS, LANES), BF),
            pltpu.VMEM((n, YS, HALF_ROWS, LANES), BF),
            pltpu.VMEM((n, YS - 1, HALF_ROWS, LANES), BF),
            pltpu.VMEM((n, HALF_ROWS, LANES), BF),
            pltpu.VMEM((n, ZS - 1, PIECE, LANES), BF),
            pltpu.VMEM((n, PIECE, LANES), BF),
            pltpu.VMEM((n - 1, PIECE, LANES), BF),
            pltpu.VMEM((CORES, YS, HALF_ROWS, LANES), BF),
            dma((7,)),
            dma((3,)),
            dma((n - 1,)), dma((n - 1,)),
            dma((n,)), dma((n,)),
            dma((3,)), dma((3,)),
            dma((1,)), dma((1,)),
            dma((n - 1,)), dma((n - 1,)),
            dma((n,)), dma((n,)),
            dma((n,)), dma((n,)),
            dma((n * (YS - 1),)), dma((n * (YS - 1),)),
            dma((n * (ZS - 1),)), dma((n * (ZS - 1),)),
            dma((n,)), dma((n - 1,)),
            dma((ZS - 1,)), dma((ZS - 1,)),
            dma((YS - 1,)), dma((YS - 1,)),
            dma((1,)), dma((1,)),
        ],
        compiler_params=pltpu.CompilerParams(
            collective_id=0, has_side_effects=True, vmem_limit_bytes=56 << 20
        ),
    )(signal, skip_cot, res_cot, w_tap, w_now, w_res, w_skip)


def solution(mesh):
    rows3 = P(None, "tm", None)
    owned = P("section", None, None)
    return jax.shard_map(
        body,
        mesh=mesh,
        in_specs=(rows3,) * 3 + (owned,) * 4,
        out_specs=(rows3, P("section", None, "tm", None)) + (owned,) * 4,
        check_vma=False,
    )
```

```python
import math

import jax
import jax.numpy as jnp
from jax import lax
from jax.experimental import pallas as pl
from jax.experimental.pallas import tpu as pltpu
from jax.sharding import PartitionSpec as P

MESH = pl.DeviceIdType.MESH
BF = jnp.bfloat16
F32 = jnp.float32

SECTIONS = 4
YS, ZS, CORES = 4, 8, 2
SHARDS = YS * ZS * CORES
ROWS, CH = 512, 256
GROUP = 16
BLOCK = ROWS // GROUP
LEAD = ROWS // 2
PARTS = 2
PART = ROWS // PARTS
HALF_ROWS = 384
PIECE = HALF_ROWS // ZS
LANES = 128


def dot(a, b):
    return jnp.dot(a, b, preferred_element_type=F32)


def dot_bt(a, b):
    return lax.dot_general(a, b, (((1,), (1,)), ((), ())), preferred_element_type=F32)


def dot_at(a, b):
    return lax.dot_general(a, b, (((0,), (0,)), ((), ())), preferred_element_type=F32)


def kernel(
    signal, skip_cot, res_cot, w_tap, w_now, w_res, w_skip,
    out_skip, out_grads, out_sums,
    wts, hp, act, sig, gated_s, skip_acc, skip_out, skip_t, cot, grad, dz, bp, part_g,
    sums, pair_r, pair_s, y_r, y_s, x_r, x_s, z_r, full,
    sem_in, sem_loc, w_ss, w_rs, wp_ss, wp_rs, in_ss, in_rs,
    skt_ss, skt_rs, skip_ss, skip_rs, ig_ss, ig_rs, s1_ss, s1_rs, s2_ss, s2_rs, s3_ss, s3_rs,
    s4_ss, s4_rs, s5_ss, s5_rs, s6_ss, s6_rs, s7_ss, s7_rs, ready,
):
    x = lax.axis_index("section")
    t = lax.axis_index("tm")
    core = lax.rem(t, CORES)
    z = lax.rem(t // CORES, ZS)
    y = t // (CORES * ZS)
    z_half, z_odd = z // 2, lax.rem(z, 2)
    me = y * 4 + z_half
    mate = t + 1 - 2 * core

    def at_x(j):
        return lax.rem(x + j + SECTIONS, SECTIONS)

    def at_y(j):
        return (lax.rem(y + j + YS, YS) * ZS + z) * CORES + core

    def at_z(j):
        return (y * ZS + lax.rem(z + j + ZS, ZS)) * CORES + core

    def member(j):
        dy, dz = j // 4, j % 4
        py, pz = lax.rem(y + dy, YS), lax.rem(z_half + dz, 4)
        return py * 4 + pz, (py * ZS + pz * 2 + z_odd) * CORES + core

    def rows(c):
        return pl.ds(c * PART, PART)

    def block(i, lead=0):
        return pl.ds(pl.multiple_of(lead + i * BLOCK, BLOCK), BLOCK)

    def remote(src, dst, ss, rs, to_x, to_t):
        return pltpu.make_async_remote_copy(
            src_ref=src, dst_ref=dst, send_sem=ss, recv_sem=rs,
            device_id=(to_x, to_t), device_id_type=MESH,
        )

    def w_copy(layer, part, way, n):
        start = core * HALF_ROWS + part * (HALF_ROWS // 2)
        here = wts.at[layer, pl.ds(pl.multiple_of(start, 64), HALF_ROWS // 2)]
        return remote(here, here, w_ss.at[n], w_rs.at[layer * 2 + part], at_x(way), t)

    def w_sends():
        return [w_copy(x, 0, 1, 0), w_copy(x, 1, -1, 1), w_copy(x, 1, 1, 2), w_copy(x, 0, -1, 3)] + [
            w_copy(at_x(-1), 0, 1, 4), w_copy(at_x(1), 1, -1, 5)
        ]

    def w_recv(layer, part):
        w_copy(layer, part, 1, 0).wait_recv()

    def w_mate(layer, whose):
        half = pl.ds(whose * HALF_ROWS, HALF_ROWS)
        return remote(
            wts.at[layer, half], wts.at[layer, half],
            wp_ss.at[layer], wp_rs.at[layer], x, mate,
        )

    inputs = (signal, skip_cot, res_cot)
    places = ((hp.at[0], LEAD), (cot, 0), (grad.at[SECTIONS], 0))

    def spread(n, j):
        place, shard = member(j)
        to, lead = places[n]
        return remote(
            inputs[n].at[x, block(place)], to.at[block(me, lead)],
            in_ss.at[n], in_rs.at[n], x, shard,
        )

    def spread_own(n):
        to, lead = places[n]
        return pltpu.make_async_copy(
            inputs[n].at[x, block(me)], to.at[block(me, lead)], sem_in.at[4 + n]
        )

    def others(ss, rs):
        some = cot.at[pl.ds(0, ROWS - BLOCK)]
        return remote(some, some, ss, rs, x, mate)

    def whole(ss, rs):
        return remote(cot, cot, ss, rs, x, mate)

    def skip_back(j):
        place, shard = member(j)
        return remote(
            skip_out.at[block(place)], skip_t.at[block(me)], skt_ss.at[0], skt_rs.at[0], x, shard
        )

    def skip_copy(j):
        return remote(
            skip_t, out_skip.at[x], skip_ss.at[j - 1], skip_rs.at[j - 1], at_x(j), t
        )

    def skip_recv(j):
        return remote(
            skip_t, out_skip.at[at_x(-j)], skip_ss.at[j - 1], skip_rs.at[j - 1], at_x(-j), t
        )

    def ig_copy(layer, j):
        place, shard = member(j)
        return remote(
            grad.at[layer, block(place)], out_grads.at[0, x, block(me)],
            ig_ss.at[layer], ig_rs.at[lax.rem(layer - x + SECTIONS, SECTIONS)], layer, shard,
        )

    def ig_own(layer):
        return pltpu.make_async_copy(
            grad.at[layer, block(me)], out_grads.at[0, x, block(me)], sem_loc.at[0]
        )

    def s1(layer):
        return remote(
            sums.at[layer, 1 - core], pair_r.at[layer],
            s1_ss.at[layer], s1_rs.at[layer], x, mate,
        )

    def s2(layer, j):
        return remote(
            pair_s.at[layer, lax.rem(y + j, YS)], y_r.at[layer, j - 1],
            s2_ss.at[layer * 3 + j - 1], s2_rs.at[layer * 3 + j - 1], x, at_y(j),
        )

    def piece(i):
        return pl.ds(pl.multiple_of(i * PIECE, 16), PIECE)

    def s3(layer):
        j = lax.rem(layer - x + SECTIONS, SECTIONS)
        return remote(
            y_s.at[layer], x_r.at[j - 1], s3_ss.at[layer], s3_rs.at[j - 1], layer, t
        )

    def s3_recv(j):
        return remote(y_s.at[0], x_r.at[j - 1], s3_ss.at[0], s3_rs.at[j - 1], at_x(-j), t)

    def s4(j):
        return remote(
            x_s.at[piece(lax.rem(z + j, ZS))], z_r.at[j - 1],
            s4_ss.at[j - 1], s4_rs.at[j - 1], x, at_z(j),
        )

    def s5(j, whose):
        return remote(
            full.at[core, y, piece(whose)], full.at[core, y, piece(whose)],
            s5_ss.at[j - 1], s5_rs.at[j - 1], x, at_z(j),
        )

    def s6(j, whose, part):
        here = full.at[core, whose, piece(part)]
        n = (j - 1) * ZS + part
        return remote(here, here, s6_ss.at[n], s6_rs.at[n], x, at_y(j))

    def s7(whose, part):
        here = full.at[core, whose, piece(part)]
        return remote(here, here, s7_ss.at[0], s7_rs.at[0], x, mate)

    def s7_all(whose):
        return remote(full.at[whose], full.at[whose], s7_ss.at[0], s7_rs.at[0], x, mate)

    loads = [
        pltpu.make_async_copy(w_tap.at[0], wts.at[x, pl.ds(0, CH)], sem_in.at[0]),
        pltpu.make_async_copy(w_now.at[0], wts.at[x, pl.ds(CH, CH)], sem_in.at[1]),
        pltpu.make_async_copy(
            w_res.at[0], wts.at[x, pl.ds(2 * CH, CH), pl.ds(0, CH)], sem_in.at[2]
        ),
        pltpu.make_async_copy(
            w_skip.at[0], wts.at[x, pl.ds(2 * CH, CH), pl.ds(CH, CH)], sem_in.at[3]
        ),
    ] + [spread_own(n) for n in range(3)]
    for load in loads:
        load.start()

    barrier = pltpu.get_barrier_semaphore()
    peers = [(x, mate)] + [(x, at_z(j)) for j in (1, 3, 5, 7)]
    peers += [(x, member(j)[1]) for j in range(1, GROUP)]
    peers += [(at_x(j), t) for j in range(1, SECTIONS)]
    for peer in peers:
        pl.semaphore_signal(barrier, inc=1, device_id=peer, device_id_type=MESH)

    for layer in range(SECTIONS):
        hp[layer, pl.ds(0, LEAD), :] = jnp.zeros((LEAD, CH), BF)
    bp[pl.ds(ROWS, LEAD), :] = jnp.zeros((LEAD, CH), BF)
    skip_acc[...] = jnp.zeros((ROWS, CH), F32)
    pl.semaphore_wait(barrier, len(peers))
    for j in range(1, SECTIONS):
        pl.semaphore_signal(ready, inc=1, device_id=(at_x(j), t), device_id_type=MESH)

    for j in range(1, GROUP):
        spread(0, j).start()
    for load in loads[:4]:
        load.wait()
    weights = w_sends()
    for copy in weights[:4]:
        copy.start()
    for n in (1, 2):
        for j in range(1, GROUP):
            spread(n, j).start()

    left, right, across = at_x(-1), at_x(1), at_x(2)
    w_recv(left, 0)
    weights[4].start()
    w_recv(right, 1)
    weights[5].start()
    w_recv(left, 1)
    w_mate(left, core).start()
    w_recv(right, 0)
    w_mate(right, core).start()
    w_recv(across, 0)
    w_recv(across, 1)
    w_mate(across, core).start()
    loads[4].wait()
    others(in_ss.at[0], in_rs.at[0]).wait_recv()

    def tap_rows(c, shift):
        return pl.ds(pl.multiple_of(LEAD + c * PART - shift, BLOCK), PART)

    def forward(k, shift):
        @pl.when(x != k)
        def _():
            w_mate(k, 1 - core).wait_recv()

        for c in range(PARTS):
            here = pl.ds(LEAD + c * PART, PART)
            h = hp[k, here, :]
            pre = dot(hp[k, tap_rows(c, shift), :], wts[k, pl.ds(0, CH), :]) + dot(
                h, wts[k, pl.ds(CH, CH), :]
            )
            a = jnp.tanh(pre[:, :CH])
            s = jax.nn.sigmoid(pre[:, CH:])
            act[k, rows(c), :] = a
            sig[k, rows(c), :] = s
            gated = (a * s).astype(BF)
            gated_s[k, rows(c), :] = gated
            out = dot(gated, wts[k, pl.ds(2 * CH, CH), :])
            skip_acc[rows(c), :] += out[:, CH:]
            hp[k + 1, here, :] = (h.astype(F32) + out[:, :CH]).astype(BF)

        return shift * 2

    lax.fori_loop(0, SECTIONS, forward, jnp.int32(BLOCK))

    skip_out[...] = skip_acc[...].astype(BF)

    def s1_to_s2(layer):
        s1(layer).wait_recv()
        pair_s[layer] = (
            sums[layer, core].astype(F32) + pair_r[layer].astype(F32)
        ).astype(BF)
        for j in range(1, YS):
            s2(layer, j).start()

    def s2_to_s3(layer):
        total = pair_s[layer, y].astype(F32)
        for j in range(1, YS):
            s2(layer, j).wait_recv()
            total = total + y_r[layer, j - 1].astype(F32)
        y_s[layer] = total.astype(BF)

        @pl.when(x != layer)
        def _():
            s3(layer).start()

    def ig_send(layer):
        @pl.when(x != layer)
        def _():
            ig_copy(layer, 0).start()

        @pl.when(x == layer)
        def _():
            ig_own(layer).start()

        for j in range(1, GROUP):
            ig_copy(layer, j).start()

    for n in (1, 2):
        loads[4 + n].wait()
        others(in_ss.at[n], in_rs.at[n]).wait_recv()
    for j in range(1, GROUP):
        skip_back(j).start()
    skip_mine = pltpu.make_async_copy(
        skip_out.at[block(me)], skip_t.at[block(me)], sem_loc.at[1]
    )
    skip_mine.start()
    pl.semaphore_wait(ready, SECTIONS - 1)

    def backward(i, shift):
        k = SECTIONS - 1 - i
        for c in range(PARTS):
            g = grad[k + 1, rows(c), :]
            du = dot_bt(g, wts[k, pl.ds(2 * CH, CH), pl.ds(0, CH)]) + dot_bt(
                cot[rows(c), :], wts[k, pl.ds(2 * CH, CH), pl.ds(CH, CH)]
            )
            a = act[k, rows(c), :]
            s = sig[k, rows(c), :]
            us = du * s
            dz[rows(c), pl.ds(0, CH)] = (us * (1.0 - a * a)).astype(BF)
            dz[rows(c), pl.ds(CH, CH)] = (us * a * (1.0 - s)).astype(BF)
            both = dot_bt(dz[rows(c), :], wts[k, pl.ds(0, 2 * CH), :])
            bp[rows(c), :] = both[:, :CH].astype(BF)
            part_g[rows(c), :] = g.astype(F32) + both[:, CH:]

        for c in range(PARTS):
            later = pl.ds(pl.multiple_of(c * PART + shift, BLOCK), PART)
            grad[k, rows(c), :] = (part_g[rows(c), :] + bp[later, :].astype(F32)).astype(BF)

        for n in range(2):
            cols = pl.ds(n * CH, CH)
            right = dz[:, cols]
            tap = hp[k, pl.ds(pl.multiple_of(LEAD - shift, BLOCK), ROWS), :]
            tap_sum = dot_at(tap, right).astype(BF)
            now_sum = dot_at(hp[k, pl.ds(LEAD, ROWS), :], right).astype(BF)
            out_sum = dot_at(gated_s[k], grad[k + 1] if n == 0 else cot[...]).astype(BF)
            rest = HALF_ROWS - CH
            if n == 0:

                ig_send(k)

            for m in range(2):
                at = 2 * n + m
                lanes = slice(m * LANES, (m + 1) * LANES)
                sums[k, 0, at, pl.ds(0, CH), :] = tap_sum[:, lanes]
                sums[k, 0, at, pl.ds(CH, rest), :] = now_sum[:rest, lanes]
                sums[k, 1, at, pl.ds(0, CH - rest), :] = now_sum[rest:, lanes]
                sums[k, 1, at, pl.ds(CH - rest, CH), :] = out_sum[:, lanes]

        @pl.when(i >= 1)
        def _():
            s1_to_s2(k + 1)

        s1(k).start()
        return shift // 2

    lax.fori_loop(0, SECTIONS, backward, jnp.int32(BLOCK << (SECTIONS - 1)))

    s1_to_s2(0)
    skip_mine.wait()
    others(skt_ss.at[0], skt_rs.at[0]).wait_recv()
    for j in range(1, SECTIONS):
        skip_copy(j).start()
    skip_own = pltpu.make_async_copy(skip_t, out_skip.at[x], sem_loc.at[2])
    skip_own.start()
    s2_to_s3(3)
    s2_to_s3(2)
    s2_to_s3(1)
    s2_to_s3(0)

    total = y_s[x].astype(F32)
    for j in range(1, SECTIONS):
        s3_recv(j).wait_recv()
        total = total + x_r[j - 1].astype(F32)
    x_s[...] = total.astype(BF)
    for j in range(1, ZS):
        s4(j).start()
    total = x_s[piece(z), :].astype(F32)
    for j in range(1, ZS):
        s4(j).wait_recv()
        total = total + z_r[j - 1].astype(F32)
    full[core, y, piece(z), :] = total.astype(BF)
    for j in range(1, ZS):
        s5(j, z).start()
    near = (0, 1, ZS - 1, 2, ZS - 2, 3, ZS - 3, 4)
    for j in near:
        part = lax.rem(z - j + ZS, ZS)
        if j:
            s5(j, part).wait_recv()
        for i in range(1, YS):
            s6(i, y, part).start()
        s7(y, part).start()
    for j in near:
        part = lax.rem(z - j + ZS, ZS)
        for i in range(1, YS):
            whose = lax.rem(y - i + YS, YS)
            s6(i, whose, part).wait_recv()
            s7(whose, part).start()
    s7_all(1 - core).wait_recv()
    done = pltpu.make_async_copy(full, out_sums, sem_loc.at[3])
    done.start()

    for copy in weights:
        copy.wait_send()
    for n in range(3):
        others(in_ss.at[n], in_rs.at[n]).wait_send()
    others(skt_ss.at[0], skt_rs.at[0]).wait_send()
    others(ig_ss.at[x], ig_rs.at[0]).wait_recv()
    others(ig_ss.at[x], ig_rs.at[0]).wait_send()
    for j in range(1, SECTIONS):
        skip_copy(j).wait_send()
        skip_recv(j).wait_recv()
        whole(ig_ss.at[0], ig_rs.at[j]).wait_recv()
    skip_own.wait()
    ig_own(x).wait()
    for j in range(1, ZS):
        s4(j).wait_send()
        s5(j, z).wait_send()
    for j in range(1, YS):
        for part in range(ZS):
            s6(j, y, part).wait_send()
    s7_all(core).wait_send()

    def drain(k, carry):
        @pl.when(x != k)
        def _():
            w_mate(k, core).wait_send()
            s3(k).wait_send()
            whole(ig_ss.at[k], ig_rs.at[0]).wait_send()

        s1(k).wait_send()
        for j in range(1, YS):
            s2(k, j).wait_send()
        return carry

    lax.fori_loop(0, SECTIONS, drain, jnp.int32(0))
    done.wait()


def finish(
    in_skip, in_grads, in_sums, out_skip, out_grads, out_tap, out_now, out_res, out_wskip,
    skip, grads, sums, tap, now, res, wskip, sem_in, sem_out,
):
    fetch = [pltpu.make_async_copy(in_sums, sums, sem_in.at[2 * SECTIONS])]
    store = []
    for i in range(SECTIONS):
        fetch.append(pltpu.make_async_copy(in_skip.at[i], skip.at[i], sem_in.at[i]))
        store.append(pltpu.make_async_copy(skip.at[i], out_skip.at[i], sem_out.at[i]))
        j = SECTIONS + i
        fetch.append(pltpu.make_async_copy(in_grads.at[0, i], grads.at[i], sem_in.at[j]))
        store.append(pltpu.make_async_copy(grads.at[i], out_grads.at[0, i], sem_out.at[j]))
    for copy in fetch:
        copy.start()
    fetch[0].wait()
    scale = 1.0 / math.sqrt(SECTIONS * ROWS * SHARDS)
    rest = HALF_ROWS - CH
    for at in range(YS):
        lanes = pl.ds(at * LANES, LANES)
        tap[:, lanes] = sums[0, at, pl.ds(0, CH), :].astype(F32) * scale
        now[pl.ds(0, rest), lanes] = sums[0, at, pl.ds(CH, rest), :].astype(F32) * scale
        now[pl.ds(rest, CH - rest), lanes] = (
            sums[1, at, pl.ds(0, CH - rest), :].astype(F32) * scale
        )
        out = res if at < 2 else wskip
        lanes = pl.ds(at % 2 * LANES, LANES)
        out[:, lanes] = sums[1, at, pl.ds(CH - rest, CH), :].astype(F32) * scale
        for i in (2 * at, 2 * at + 1):
            fetch[1 + i].wait()
            store[i].start()
    pairs = ((tap, out_tap), (now, out_now), (res, out_res), (wskip, out_wskip))
    for i, (got, to) in enumerate(pairs):
        store.append(pltpu.make_async_copy(got, to.at[0], sem_out.at[2 * SECTIONS + i]))
        store[-1].start()
    for copy in store:
        copy.wait()


def body(signal, skip_cot, res_cot, w_tap, w_now, w_res, w_skip):
    any_space = pl.BlockSpec(memory_space=pl.ANY)
    dma = pltpu.SemaphoreType.DMA
    n = SECTIONS
    gathered = pl.pallas_call(
        kernel,
        out_shape=(
            jax.ShapeDtypeStruct((n, ROWS, CH), BF),
            jax.ShapeDtypeStruct((1, n, ROWS, CH), BF),
            jax.ShapeDtypeStruct((CORES, YS, HALF_ROWS, LANES), BF),
        ),
        in_specs=[any_space] * 7,
        out_specs=(any_space,) * 3,
        scratch_shapes=[
            pltpu.VMEM((n, 3 * CH, 2 * CH), BF),
            pltpu.VMEM((n + 1, LEAD + ROWS, CH), BF),
            pltpu.VMEM((n, ROWS, CH), F32),
            pltpu.VMEM((n, ROWS, CH), F32),
            pltpu.VMEM((n, ROWS, CH), BF),
            pltpu.VMEM((ROWS, CH), F32),
            pltpu.VMEM((ROWS, CH), BF),
            pltpu.VMEM((ROWS, CH), BF),
            pltpu.VMEM((ROWS, CH), BF),
            pltpu.VMEM((n + 1, ROWS, CH), BF),
            pltpu.VMEM((ROWS, 2 * CH), BF),
            pltpu.VMEM((ROWS + LEAD, CH), BF),
            pltpu.VMEM((ROWS, CH), F32),
            pltpu.VMEM((n, CORES, YS, HALF_ROWS, LANES), BF),
            pltpu.VMEM((n, YS, HALF_ROWS, LANES), BF),
            pltpu.VMEM((n, YS, HALF_ROWS, LANES), BF),
            pltpu.VMEM((n, YS - 1, HALF_ROWS, LANES), BF),
            pltpu.VMEM((n, HALF_ROWS, LANES), BF),
            pltpu.VMEM((n - 1, HALF_ROWS, LANES), BF),
            pltpu.VMEM((HALF_ROWS, LANES), BF),
            pltpu.VMEM((ZS - 1, PIECE, LANES), BF),
            pltpu.VMEM((CORES, YS, HALF_ROWS, LANES), BF),
            dma((7,)),
            dma((4,)),
            dma((6,)), dma((2 * n,)),
            dma((n,)), dma((n,)),
            dma((3,)), dma((3,)),
            dma((1,)), dma((1,)),
            dma((n - 1,)), dma((n - 1,)),
            dma((n,)), dma((n,)),
            dma((n,)), dma((n,)),
            dma((n * (YS - 1),)), dma((n * (YS - 1),)),
            dma((n,)), dma((n - 1,)),
            dma((ZS - 1,)), dma((ZS - 1,)),
            dma((ZS - 1,)), dma((ZS - 1,)),
            dma(((YS - 1) * ZS,)), dma(((YS - 1) * ZS,)),
            dma((1,)), dma((1,)),
            pltpu.SemaphoreType.REGULAR,
        ],
        compiler_params=pltpu.CompilerParams(
            collective_id=0, has_side_effects=True, vmem_limit_bytes=56 << 20
        ),
    )(signal, skip_cot, res_cot, w_tap, w_now, w_res, w_skip)
    return pl.pallas_call(
        finish,
        out_shape=(
            jax.ShapeDtypeStruct((n, ROWS, CH), BF),
            jax.ShapeDtypeStruct((1, n, ROWS, CH), BF),
            jax.ShapeDtypeStruct((1, CH, 2 * CH), F32),
            jax.ShapeDtypeStruct((1, CH, 2 * CH), F32),
            jax.ShapeDtypeStruct((1, CH, CH), F32),
            jax.ShapeDtypeStruct((1, CH, CH), F32),
        ),
        in_specs=[any_space] * 3,
        out_specs=(any_space,) * 6,
        scratch_shapes=[
            pltpu.VMEM((n, ROWS, CH), BF),
            pltpu.VMEM((n, ROWS, CH), BF),
            pltpu.VMEM((CORES, YS, HALF_ROWS, LANES), BF),
            pltpu.VMEM((CH, 2 * CH), F32),
            pltpu.VMEM((CH, 2 * CH), F32),
            pltpu.VMEM((CH, CH), F32),
            pltpu.VMEM((CH, CH), F32),
            dma((2 * n + 1,)),
            dma((2 * n + 4,)),
        ],
        compiler_params=pltpu.CompilerParams(vmem_limit_bytes=56 << 20),
    )(*gathered)


def solution(mesh):
    rows3 = P(None, "tm", None)
    owned = P("section", None, None)
    return jax.shard_map(
        body,
        mesh=mesh,
        in_specs=(rows3,) * 3 + (owned,) * 4,
        out_specs=(rows3, P("section", None, "tm", None)) + (owned,) * 4,
        check_vma=False,
    )
```

```python
import math

import jax
import jax.numpy as jnp
from jax import lax
from jax.experimental import pallas as pl
from jax.experimental.pallas import tpu as pltpu
from jax.sharding import PartitionSpec as P

MESH = pl.DeviceIdType.MESH
BF = jnp.bfloat16
F32 = jnp.float32

SECTIONS = 4
YS, ZS, CORES = 4, 8, 2
SHARDS = YS * ZS * CORES
ROWS, CH = 512, 256
GROUP = 16
ORDER = (1, 3, 4, 12, 5, 15, 7, 13, 2, 8, 9, 11, 6, 14, 10)
BLOCK = ROWS // GROUP
LEAD = ROWS // 2
PARTS = 2
PART = ROWS // PARTS
HALF_ROWS = 384
PIECE = HALF_ROWS // ZS
LANES = 128


def dot(a, b):
    return jnp.dot(a, b, preferred_element_type=F32)


def dot_bt(a, b):
    return lax.dot_general(a, b, (((1,), (1,)), ((), ())), preferred_element_type=F32)


def dot_at(a, b):
    return lax.dot_general(a, b, (((0,), (0,)), ((), ())), preferred_element_type=F32)


def kernel(
    signal, skip_cot, res_cot, w_tap, w_now, w_res, w_skip,
    out_skip, out_grads, out_sums,
    wts, hp, act, sig, gated_s, skip_acc, skip_out, skip_t, cot, grad, dz, bp, part_g,
    sums, pair_r, pair_s, y_r, y_s, z_r, z_s, x_r, full,
    sem_in, sem_loc, w_ss, w_rs, wp_ss, wp_rs, in_ss, in_rs,
    skt_ss, skt_rs, skip_ss, skip_rs, ig_ss, ig_rs, s1_ss, s1_rs, s2_ss, s2_rs, s3_ss, s3_rs,
    s4_ss, s4_rs, s5_ss, s5_rs, s6_ss, s6_rs, s7_ss, s7_rs, ready,
):
    x = lax.axis_index("section")
    t = lax.axis_index("tm")
    core = lax.rem(t, CORES)
    z = lax.rem(t // CORES, ZS)
    y = t // (CORES * ZS)
    z_half, z_odd = z // 2, lax.rem(z, 2)
    me = y * 4 + z_half
    mate = t + 1 - 2 * core

    def at_x(j):
        return lax.rem(x + j + SECTIONS, SECTIONS)

    def at_y(j):
        return (lax.rem(y + j + YS, YS) * ZS + z) * CORES + core

    def at_z(j):
        return (y * ZS + lax.rem(z + j + ZS, ZS)) * CORES + core

    def member(j):
        dy, dz = j // 4, j % 4
        py, pz = lax.rem(y + dy, YS), lax.rem(z_half + dz, 4)
        return py * 4 + pz, (py * ZS + pz * 2 + z_odd) * CORES + core

    def rows(c):
        return pl.ds(c * PART, PART)

    def block(i, lead=0):
        return pl.ds(pl.multiple_of(lead + i * BLOCK, BLOCK), BLOCK)

    def remote(src, dst, ss, rs, to_x, to_t):
        return pltpu.make_async_remote_copy(
            src_ref=src, dst_ref=dst, send_sem=ss, recv_sem=rs,
            device_id=(to_x, to_t), device_id_type=MESH,
        )

    def w_copy(layer, part, way, n):
        start = core * HALF_ROWS + part * (HALF_ROWS // 2)
        here = wts.at[layer, pl.ds(pl.multiple_of(start, 64), HALF_ROWS // 2)]
        return remote(here, here, w_ss.at[n], w_rs.at[layer * 2 + part], at_x(way), t)

    def w_sends():
        return [w_copy(x, 0, 1, 0), w_copy(x, 1, -1, 1), w_copy(x, 1, 1, 2), w_copy(x, 0, -1, 3)] + [
            w_copy(at_x(-1), 0, 1, 4), w_copy(at_x(1), 1, -1, 5)
        ]

    def w_recv(layer, part):
        w_copy(layer, part, 1, 0).wait_recv()

    def w_mate(layer, whose):
        half = pl.ds(whose * HALF_ROWS, HALF_ROWS)
        return remote(
            wts.at[layer, half], wts.at[layer, half],
            wp_ss.at[layer], wp_rs.at[layer], x, mate,
        )

    inputs = (signal, skip_cot, res_cot)
    places = ((hp.at[0], LEAD), (cot, 0), (grad.at[SECTIONS], 0))

    def spread(n, j):
        place, shard = member(j)
        to, lead = places[n]
        return remote(
            inputs[n].at[x, block(place)], to.at[block(me, lead)],
            in_ss.at[n], in_rs.at[n], x, shard,
        )

    def spread_own(n):
        to, lead = places[n]
        return pltpu.make_async_copy(
            inputs[n].at[x, block(me)], to.at[block(me, lead)], sem_in.at[4 + n]
        )

    def others(ss, rs):
        some = cot.at[pl.ds(0, ROWS - BLOCK)]
        return remote(some, some, ss, rs, x, mate)

    def whole(ss, rs):
        return remote(cot, cot, ss, rs, x, mate)

    def skip_back(j):
        place, shard = member(j)
        return remote(
            skip_out.at[block(place)], skip_t.at[block(me)], skt_ss.at[0], skt_rs.at[0], x, shard
        )

    def skip_copy(j):
        return remote(
            skip_t, out_skip.at[x], skip_ss.at[j - 1], skip_rs.at[j - 1], at_x(j), t
        )

    def skip_recv(j):
        return remote(
            skip_t, out_skip.at[at_x(-j)], skip_ss.at[j - 1], skip_rs.at[j - 1], at_x(-j), t
        )

    def ig_copy(layer, j):
        place, shard = member(j)
        return remote(
            grad.at[layer, block(place)], out_grads.at[0, x, block(me)],
            ig_ss.at[layer], ig_rs.at[lax.rem(layer - x + SECTIONS, SECTIONS)], layer, shard,
        )

    def ig_own(layer):
        return pltpu.make_async_copy(
            grad.at[layer, block(me)], out_grads.at[0, x, block(me)], sem_loc.at[0]
        )

    def s1(layer):
        return remote(
            sums.at[layer, 1 - core], pair_r.at[layer],
            s1_ss.at[layer], s1_rs.at[layer], x, mate,
        )

    def s2(layer, j):
        return remote(
            pair_s.at[layer, lax.rem(y + j, YS)], y_r.at[layer, j - 1],
            s2_ss.at[layer * 3 + j - 1], s2_rs.at[layer * 3 + j - 1], x, at_y(j),
        )

    def piece(i):
        return pl.ds(pl.multiple_of(i * PIECE, 16), PIECE)

    def s3(layer, j):
        return remote(
            y_s.at[layer, piece(lax.rem(z + j, ZS))], z_r.at[layer, j - 1],
            s3_ss.at[layer * 7 + j - 1], s3_rs.at[layer * 7 + j - 1], x, at_z(j),
        )

    def s4(layer):
        j = lax.rem(layer - x + SECTIONS, SECTIONS)
        return remote(
            z_s.at[layer], x_r.at[j - 1], s4_ss.at[layer], s4_rs.at[j - 1], layer, t
        )

    def s4_recv(j):
        return remote(z_s.at[0], x_r.at[j - 1], s4_ss.at[0], s4_rs.at[j - 1], at_x(-j), t)

    def s5(j, whose):
        return remote(
            full.at[core, y, piece(whose)], full.at[core, y, piece(whose)],
            s5_ss.at[j - 1], s5_rs.at[j - 1], x, at_z(j),
        )

    def s6(j, whose, part):
        here = full.at[core, whose, piece(part)]
        n = (j - 1) * ZS + part
        return remote(here, here, s6_ss.at[n], s6_rs.at[n], x, at_y(j))

    def s7(whose, part):
        here = full.at[core, whose, piece(part)]
        return remote(here, here, s7_ss.at[0], s7_rs.at[0], x, mate)

    def s7_all(whose):
        return remote(full.at[whose], full.at[whose], s7_ss.at[0], s7_rs.at[0], x, mate)

    loads = [
        pltpu.make_async_copy(w_tap.at[0], wts.at[x, pl.ds(0, CH)], sem_in.at[0]),
        pltpu.make_async_copy(w_now.at[0], wts.at[x, pl.ds(CH, CH)], sem_in.at[1]),
        pltpu.make_async_copy(
            w_res.at[0], wts.at[x, pl.ds(2 * CH, CH), pl.ds(0, CH)], sem_in.at[2]
        ),
        pltpu.make_async_copy(
            w_skip.at[0], wts.at[x, pl.ds(2 * CH, CH), pl.ds(CH, CH)], sem_in.at[3]
        ),
    ] + [spread_own(n) for n in range(3)]
    for load in loads:
        load.start()

    barrier = pltpu.get_barrier_semaphore()
    peers = [(x, mate)] + [(x, at_z(j)) for j in (1, 3, 5, 7)]
    peers += [(x, member(j)[1]) for j in ORDER]
    peers += [(at_x(j), t) for j in range(1, SECTIONS)]
    for peer in peers:
        pl.semaphore_signal(barrier, inc=1, device_id=peer, device_id_type=MESH)

    for layer in range(SECTIONS):
        hp[layer, pl.ds(0, LEAD), :] = jnp.zeros((LEAD, CH), BF)
    bp[pl.ds(ROWS, LEAD), :] = jnp.zeros((LEAD, CH), BF)
    skip_acc[...] = jnp.zeros((ROWS, CH), F32)
    pl.semaphore_wait(barrier, len(peers))
    for j in range(1, SECTIONS):
        pl.semaphore_signal(ready, inc=1, device_id=(at_x(j), t), device_id_type=MESH)

    for j in ORDER:
        spread(0, j).start()
    for load in loads[:4]:
        load.wait()
    weights = w_sends()
    for copy in weights[:4]:
        copy.start()
    for n in (1, 2):
        for j in ORDER:
            spread(n, j).start()

    left, right, across = at_x(-1), at_x(1), at_x(2)
    w_recv(left, 0)
    weights[4].start()
    w_recv(right, 1)
    weights[5].start()
    w_recv(left, 1)
    w_mate(left, core).start()
    w_recv(right, 0)
    w_mate(right, core).start()
    w_recv(across, 0)
    w_recv(across, 1)
    w_mate(across, core).start()
    loads[4].wait()
    others(in_ss.at[0], in_rs.at[0]).wait_recv()

    def tap_rows(c, shift):
        return pl.ds(pl.multiple_of(LEAD + c * PART - shift, BLOCK), PART)

    def forward(k, shift):
        @pl.when(x != k)
        def _():
            w_mate(k, 1 - core).wait_recv()

        for c in range(PARTS):
            here = pl.ds(LEAD + c * PART, PART)
            h = hp[k, here, :]
            pre = dot(hp[k, tap_rows(c, shift), :], wts[k, pl.ds(0, CH), :]) + dot(
                h, wts[k, pl.ds(CH, CH), :]
            )
            a = jnp.tanh(pre[:, :CH])
            s = jax.nn.sigmoid(pre[:, CH:])
            act[k, rows(c), :] = a
            sig[k, rows(c), :] = s
            gated = (a * s).astype(BF)
            gated_s[k, rows(c), :] = gated
            out = dot(gated, wts[k, pl.ds(2 * CH, CH), :])
            skip_acc[rows(c), :] += out[:, CH:]
            hp[k + 1, here, :] = (h.astype(F32) + out[:, :CH]).astype(BF)

        return shift * 2

    lax.fori_loop(0, SECTIONS, forward, jnp.int32(BLOCK))

    skip_out[...] = skip_acc[...].astype(BF)
    for j in ORDER:
        skip_back(j).start()
    skip_mine = pltpu.make_async_copy(
        skip_out.at[block(me)], skip_t.at[block(me)], sem_loc.at[1]
    )
    skip_mine.start()

    def s1_to_s2(layer):
        s1(layer).wait_recv()
        pair_s[layer] = (
            sums[layer, core].astype(F32) + pair_r[layer].astype(F32)
        ).astype(BF)
        for j in range(1, YS):
            s2(layer, j).start()

    def s2_to_s3(layer):
        total = pair_s[layer, y].astype(F32)
        for j in range(1, YS):
            s2(layer, j).wait_recv()
            total = total + y_r[layer, j - 1].astype(F32)
        y_s[layer] = total.astype(BF)
        for j in range(1, ZS):
            s3(layer, j).start()

    def s3_to_s4(layer):
        total = y_s[layer, piece(z), :].astype(F32)
        for j in range(1, ZS):
            s3(layer, j).wait_recv()
            total = total + z_r[layer, j - 1].astype(F32)
        z_s[layer] = total.astype(BF)

        @pl.when(x != layer)
        def _():
            s4(layer).start()

    for n in (1, 2):
        loads[4 + n].wait()
        others(in_ss.at[n], in_rs.at[n]).wait_recv()
    pl.semaphore_wait(ready, SECTIONS - 1)

    def backward(i, shift):
        k = SECTIONS - 1 - i
        for c in range(PARTS):
            g = grad[k + 1, rows(c), :]
            du = dot_bt(g, wts[k, pl.ds(2 * CH, CH), pl.ds(0, CH)]) + dot_bt(
                cot[rows(c), :], wts[k, pl.ds(2 * CH, CH), pl.ds(CH, CH)]
            )
            a = act[k, rows(c), :]
            s = sig[k, rows(c), :]
            us = du * s
            dz[rows(c), pl.ds(0, CH)] = (us * (1.0 - a * a)).astype(BF)
            dz[rows(c), pl.ds(CH, CH)] = (us * a * (1.0 - s)).astype(BF)
            both = dot_bt(dz[rows(c), :], wts[k, pl.ds(0, 2 * CH), :])
            bp[rows(c), :] = both[:, :CH].astype(BF)
            part_g[rows(c), :] = g.astype(F32) + both[:, CH:]

        for c in range(PARTS):
            later = pl.ds(pl.multiple_of(c * PART + shift, BLOCK), PART)
            grad[k, rows(c), :] = (part_g[rows(c), :] + bp[later, :].astype(F32)).astype(BF)

        for n in range(2):
            cols = pl.ds(n * CH, CH)
            right = dz[:, cols]
            tap = hp[k, pl.ds(pl.multiple_of(LEAD - shift, BLOCK), ROWS), :]
            tap_sum = dot_at(tap, right).astype(BF)
            now_sum = dot_at(hp[k, pl.ds(LEAD, ROWS), :], right).astype(BF)
            out_sum = dot_at(gated_s[k], grad[k + 1] if n == 0 else cot[...]).astype(BF)
            rest = HALF_ROWS - CH
            if n == 0:
                @pl.when(x != k)
                def _():
                    ig_copy(k, 0).start()

                @pl.when(x == k)
                def _():
                    ig_own(k).start()

                for j in ORDER:
                    ig_copy(k, j).start()

            for m in range(2):
                at = 2 * n + m
                lanes = slice(m * LANES, (m + 1) * LANES)
                sums[k, 0, at, pl.ds(0, CH), :] = tap_sum[:, lanes]
                sums[k, 0, at, pl.ds(CH, rest), :] = now_sum[:rest, lanes]
                sums[k, 1, at, pl.ds(0, CH - rest), :] = now_sum[rest:, lanes]
                sums[k, 1, at, pl.ds(CH - rest, CH), :] = out_sum[:, lanes]
        s1(k).start()

        @pl.when(i >= 1)
        def _():
            s1_to_s2(k + 1)

        return shift // 2

    lax.fori_loop(0, SECTIONS, backward, jnp.int32(BLOCK << (SECTIONS - 1)))

    s1_to_s2(0)
    skip_mine.wait()
    others(skt_ss.at[0], skt_rs.at[0]).wait_recv()
    for j in range(1, SECTIONS):
        skip_copy(j).start()
    skip_own = pltpu.make_async_copy(skip_t, out_skip.at[x], sem_loc.at[2])
    skip_own.start()
    s2_to_s3(3)
    s2_to_s3(2)
    s3_to_s4(3)
    s2_to_s3(1)
    s3_to_s4(2)
    s2_to_s3(0)
    s3_to_s4(1)
    s3_to_s4(0)

    total = z_s[x].astype(F32)
    for j in range(1, SECTIONS):
        s4_recv(j).wait_recv()
        total = total + x_r[j - 1].astype(F32)
    full[core, y, piece(z), :] = total.astype(BF)
    for j in range(1, ZS):
        s5(j, z).start()
    near = (0, 1, ZS - 1, 2, ZS - 2, 3, ZS - 3, 4)
    for j in near:
        part = lax.rem(z - j + ZS, ZS)
        if j:
            s5(j, part).wait_recv()
        for i in range(1, YS):
            s6(i, y, part).start()
        s7(y, part).start()
    for j in near:
        part = lax.rem(z - j + ZS, ZS)
        for i in range(1, YS):
            whose = lax.rem(y - i + YS, YS)
            s6(i, whose, part).wait_recv()
            s7(whose, part).start()
    s7_all(1 - core).wait_recv()
    done = pltpu.make_async_copy(full, out_sums, sem_loc.at[3])
    done.start()

    for copy in weights:
        copy.wait_send()
    for n in range(3):
        others(in_ss.at[n], in_rs.at[n]).wait_send()
    others(skt_ss.at[0], skt_rs.at[0]).wait_send()
    others(ig_ss.at[x], ig_rs.at[0]).wait_recv()
    others(ig_ss.at[x], ig_rs.at[0]).wait_send()
    for j in range(1, SECTIONS):
        skip_copy(j).wait_send()
        skip_recv(j).wait_recv()
        whole(ig_ss.at[0], ig_rs.at[j]).wait_recv()
    skip_own.wait()
    ig_own(x).wait()
    for j in range(1, ZS):
        s5(j, z).wait_send()
    for j in range(1, YS):
        for part in range(ZS):
            s6(j, y, part).wait_send()
    s7_all(core).wait_send()

    def drain(k, carry):
        @pl.when(x != k)
        def _():
            w_mate(k, core).wait_send()
            s4(k).wait_send()
            whole(ig_ss.at[k], ig_rs.at[0]).wait_send()

        s1(k).wait_send()
        for j in range(1, YS):
            s2(k, j).wait_send()
        for j in range(1, ZS):
            s3(k, j).wait_send()
        return carry

    lax.fori_loop(0, SECTIONS, drain, jnp.int32(0))
    done.wait()


def finish(
    in_skip, in_grads, in_sums, out_skip, out_grads, out_tap, out_now, out_res, out_wskip,
    skip, grads, sums, tap, now, res, wskip, sem_in, sem_out,
):
    fetch = [pltpu.make_async_copy(in_sums, sums, sem_in.at[2 * SECTIONS])]
    store = []
    for i in range(SECTIONS):
        fetch.append(pltpu.make_async_copy(in_skip.at[i], skip.at[i], sem_in.at[i]))
        store.append(pltpu.make_async_copy(skip.at[i], out_skip.at[i], sem_out.at[i]))
        j = SECTIONS + i
        fetch.append(pltpu.make_async_copy(in_grads.at[0, i], grads.at[i], sem_in.at[j]))
        store.append(pltpu.make_async_copy(grads.at[i], out_grads.at[0, i], sem_out.at[j]))
    for copy in fetch:
        copy.start()
    fetch[0].wait()
    scale = 1.0 / math.sqrt(SECTIONS * ROWS * SHARDS)
    rest = HALF_ROWS - CH
    for at in range(YS):
        lanes = pl.ds(at * LANES, LANES)
        tap[:, lanes] = sums[0, at, pl.ds(0, CH), :].astype(F32) * scale
        now[pl.ds(0, rest), lanes] = sums[0, at, pl.ds(CH, rest), :].astype(F32) * scale
        now[pl.ds(rest, CH - rest), lanes] = (
            sums[1, at, pl.ds(0, CH - rest), :].astype(F32) * scale
        )
        out = res if at < 2 else wskip
        lanes = pl.ds(at % 2 * LANES, LANES)
        out[:, lanes] = sums[1, at, pl.ds(CH - rest, CH), :].astype(F32) * scale
        for i in (2 * at, 2 * at + 1):
            fetch[1 + i].wait()
            store[i].start()
    pairs = ((tap, out_tap), (now, out_now), (res, out_res), (wskip, out_wskip))
    for i, (got, to) in enumerate(pairs):
        store.append(pltpu.make_async_copy(got, to.at[0], sem_out.at[2 * SECTIONS + i]))
        store[-1].start()
    for copy in store:
        copy.wait()


def body(signal, skip_cot, res_cot, w_tap, w_now, w_res, w_skip):
    any_space = pl.BlockSpec(memory_space=pl.ANY)
    dma = pltpu.SemaphoreType.DMA
    n = SECTIONS
    gathered = pl.pallas_call(
        kernel,
        out_shape=(
            jax.ShapeDtypeStruct((n, ROWS, CH), BF),
            jax.ShapeDtypeStruct((1, n, ROWS, CH), BF),
            jax.ShapeDtypeStruct((CORES, YS, HALF_ROWS, LANES), BF),
        ),
        in_specs=[any_space] * 7,
        out_specs=(any_space,) * 3,
        scratch_shapes=[
            pltpu.VMEM((n, 3 * CH, 2 * CH), BF),
            pltpu.VMEM((n + 1, LEAD + ROWS, CH), BF),
            pltpu.VMEM((n, ROWS, CH), F32),
            pltpu.VMEM((n, ROWS, CH), F32),
            pltpu.VMEM((n, ROWS, CH), BF),
            pltpu.VMEM((ROWS, CH), F32),
            pltpu.VMEM((ROWS, CH), BF),
            pltpu.VMEM((ROWS, CH), BF),
            pltpu.VMEM((ROWS, CH), BF),
            pltpu.VMEM((n + 1, ROWS, CH), BF),
            pltpu.VMEM((ROWS, 2 * CH), BF),
            pltpu.VMEM((ROWS + LEAD, CH), BF),
            pltpu.VMEM((ROWS, CH), F32),
            pltpu.VMEM((n, CORES, YS, HALF_ROWS, LANES), BF),
            pltpu.VMEM((n, YS, HALF_ROWS, LANES), BF),
            pltpu.VMEM((n, YS, HALF_ROWS, LANES), BF),
            pltpu.VMEM((n, YS - 1, HALF_ROWS, LANES), BF),
            pltpu.VMEM((n, HALF_ROWS, LANES), BF),
            pltpu.VMEM((n, ZS - 1, PIECE, LANES), BF),
            pltpu.VMEM((n, PIECE, LANES), BF),
            pltpu.VMEM((n - 1, PIECE, LANES), BF),
            pltpu.VMEM((CORES, YS, HALF_ROWS, LANES), BF),
            dma((7,)),
            dma((4,)),
            dma((6,)), dma((2 * n,)),
            dma((n,)), dma((n,)),
            dma((3,)), dma((3,)),
            dma((1,)), dma((1,)),
            dma((n - 1,)), dma((n - 1,)),
            dma((n,)), dma((n,)),
            dma((n,)), dma((n,)),
            dma((n * (YS - 1),)), dma((n * (YS - 1),)),
            dma((n * (ZS - 1),)), dma((n * (ZS - 1),)),
            dma((n,)), dma((n - 1,)),
            dma((ZS - 1,)), dma((ZS - 1,)),
            dma(((YS - 1) * ZS,)), dma(((YS - 1) * ZS,)),
            dma((1,)), dma((1,)),
            pltpu.SemaphoreType.REGULAR,
        ],
        compiler_params=pltpu.CompilerParams(
            collective_id=0, has_side_effects=True, vmem_limit_bytes=56 << 20
        ),
    )(signal, skip_cot, res_cot, w_tap, w_now, w_res, w_skip)
    return pl.pallas_call(
        finish,
        out_shape=(
            jax.ShapeDtypeStruct((n, ROWS, CH), BF),
            jax.ShapeDtypeStruct((1, n, ROWS, CH), BF),
            jax.ShapeDtypeStruct((1, CH, 2 * CH), F32),
            jax.ShapeDtypeStruct((1, CH, 2 * CH), F32),
            jax.ShapeDtypeStruct((1, CH, CH), F32),
            jax.ShapeDtypeStruct((1, CH, CH), F32),
        ),
        in_specs=[any_space] * 3,
        out_specs=(any_space,) * 6,
        scratch_shapes=[
            pltpu.VMEM((n, ROWS, CH), BF),
            pltpu.VMEM((n, ROWS, CH), BF),
            pltpu.VMEM((CORES, YS, HALF_ROWS, LANES), BF),
            pltpu.VMEM((CH, 2 * CH), F32),
            pltpu.VMEM((CH, 2 * CH), F32),
            pltpu.VMEM((CH, CH), F32),
            pltpu.VMEM((CH, CH), F32),
            dma((2 * n + 1,)),
            dma((2 * n + 4,)),
        ],
        compiler_params=pltpu.CompilerParams(vmem_limit_bytes=56 << 20),
    )(*gathered)


def solution(mesh):
    rows3 = P(None, "tm", None)
    owned = P("section", None, None)
    return jax.shard_map(
        body,
        mesh=mesh,
        in_specs=(rows3,) * 3 + (owned,) * 4,
        out_specs=(rows3, P("section", None, "tm", None)) + (owned,) * 4,
        check_vma=False,
    )
```
